128 devices in a mesh: gx: 8 (over y, x_hi), gy: 4 (over x_lo, core), gz: 4 (over z).
Axes of the slice: x: 4 (x_hi: 2, x_lo: 2; x = x_hi * 2 + x_lo), y: 4, z: 4, core: 2. Of those that a mesh axis runs over, the one named last changes fastest.
Arguments:
- field: float32 [1024, 256, 512], P('gx', 'gy', 'gz'), may hold values from -1 to 1, as said below
- start_basis: float32 [1024, 128], replicated, may hold values from -6 to 6
Outputs:
- scaled_basis: float32 [1024, 128], P('gx')
- core: float32 [128, 256, 512], P('gx', 'gy', 'gz')
The draws below stay inside these ranges and needn't reach their ends.
Inputs may be any that keep to these rules, and one draw needn't show every extreme that they name: `field`: real values of varying scale over rows and columns.
All inputs are finite; a program needn't handle non-finite values.
Results may differ from the reference program's by a relative error of at most 0.00027.
Values sent between devices are 32-bit elements; how exact they have to be, the bound alone decides.
A program may use at most 64 MiB of HBM per device.

```python
import math
import jax
import jax.numpy as jnp
from jax import lax

NX = 1024
RANK = 128
ITERS = 8
NY = 256
NZ = 512


def draw_field(key, part):
    keys = jax.random.split(jax.random.fold_in(key, 17), 3)
    row_scale = jnp.exp(jax.random.uniform(keys[0], (NX, 1, 1), jnp.float32, 0.0, math.log(4.0)))
    base = jnp.clip(jax.random.normal(keys[2], (NX, NY, NZ), jnp.float32), -5.0, 5.0)
    col_scale = jnp.exp(jax.random.uniform(keys[1], (1, NY, NZ), jnp.float32, 0.0, math.log(10.0)))
    values = base * row_scale * col_scale * (0.125 / math.sqrt(NX)) * 0.75
    return jnp.clip(values, -1.0, 1.0).astype(jnp.float32)


def scatter_about(own_key, shape, width, bound, kind=jnp.bfloat16):
    array = jax.random.normal(own_key, shape, jnp.float32) * width
    return jnp.minimum(jnp.maximum(array, -bound), bound).astype(kind)


def setup_inputs(seed: int = 0) -> dict:
    seeds = jax.random.split(jax.random.key(seed), 3)
    field = draw_field(jax.random.fold_in(seeds[2], 71), 0)
    start_basis = scatter_about(seeds[1], (NX, RANK), 1.0, 6.0, jnp.float32)
    return {"field": field, "start_basis": start_basis}


def reference(field, start_basis):
    hi = lax.Precision.HIGHEST
    unfolded = field.reshape(NX, NY * NZ)
    gram = jnp.dot(unfolded.astype(jnp.float32), unfolded.T.astype(jnp.float32), precision=hi, preferred_element_type=jnp.float32)
    basis = start_basis
    for step in range(ITERS):
        image = jnp.dot(gram.astype(jnp.float32), basis.astype(jnp.float32), precision=hi, preferred_element_type=jnp.float32)
        small = jnp.dot(image.T.astype(jnp.float32), image.astype(jnp.float32), precision=hi, preferred_element_type=jnp.float32)
        lower = jnp.linalg.cholesky(small)
        basis = lax.linalg.triangular_solve(lower, image, left_side=False, lower=True, transpose_a=True)
    scaled_basis = basis * jnp.sqrt(jnp.float32(NX))
    core = jnp.dot(basis.T.astype(jnp.float32), unfolded.astype(jnp.float32), precision=hi, preferred_element_type=jnp.float32)
    return (scaled_basis, core.reshape(RANK, NY, NZ))
```

```python
import functools

import jax
import jax.numpy as jnp
from jax import lax
from jax.experimental import pallas as pl
from jax.experimental.pallas import tpu as pltpu
from jax.sharding import PartitionSpec as P

ITERS = 8
F32 = jnp.float32
BF16 = jnp.bfloat16


def split(x):
    high = x.astype(BF16)
    return high, (x - high.astype(F32)).astype(BF16)


def dg(a, b, ca, cb):
    return lax.dot_general(a, b, (((ca,), (cb,)), ((), ())), preferred_element_type=F32)


def lower_inverse(aug, panel=8):
    n = aug.shape[0]
    row = lax.broadcasted_iota(jnp.int32, (panel, n), 0)
    for first in range(0, n, panel):
        left, right = aug[first : first + panel, :n], aug[first : first + panel, n:]
        cols = [jnp.broadcast_to(left[:, first + k : first + k + 1], (panel, n)) for k in range(panel)]
        pivots = None
        for i in range(panel):
            pivot = jnp.broadcast_to(cols[i][i : i + 1, :], (panel, n))
            ratio = jnp.where(row > i, cols[i], 0.0) * (1.0 / pivot)
            for k in range(i + 1, panel):
                cols[k] = cols[k] - ratio * jnp.broadcast_to(cols[k][i : i + 1, :], (panel, n))
            left = left - ratio * jnp.broadcast_to(left[i : i + 1, :], (panel, n))
            right = right - ratio * jnp.broadcast_to(right[i : i + 1, :], (panel, n))
            pivots = pivot if pivots is None else jnp.where(row == i, pivot, pivots)
        scale = lax.rsqrt(pivots)
        left, right = left * scale, right * scale
        aug[first : first + panel, n:] = right
        if first + panel < n:
            update = lax.dot_general(
                left,
                jnp.concatenate([left, right], axis=1),
                (((0,), (0,)), ((), ())),
                precision=lax.Precision.HIGHEST,
                preferred_element_type=F32,
            )
            aug[first + panel :, :] = aug[first + panel :, :] - update[first + panel :, :]


def iteration_kernel(gram_ref, start_ref, out_ref, gram_high, gram_low, aug, basis):
    high, low = split(gram_ref[...])
    gram_high[...] = high
    gram_low[...] = low
    basis[...] = start_ref[...]
    n = aug.shape[0]
    shape = (n, n)
    eye = (lax.broadcasted_iota(jnp.int32, shape, 0) == lax.broadcasted_iota(jnp.int32, shape, 1)).astype(F32)

    def step(_, carry):
        bh, bl = split(basis[...])
        both = dg(gram_high[...], jnp.concatenate([bh, bl], axis=1), 1, 0)
        image = both[:, :n] + both[:, n:] + dg(gram_low[...], bh, 1, 0)
        ih, il = split(image)
        both = dg(ih, jnp.concatenate([ih, il], axis=1), 0, 0)
        mixed = both[:, n:]
        aug[:, :n] = both[:, :n] + mixed + mixed.T
        aug[:, n:] = eye
        lower_inverse(aug)
        th, tl = split(aug[:, n:])
        both = dg(ih, jnp.concatenate([th, tl], axis=0), 1, 1)
        basis[...] = both[:, :n] + both[:, n:] + dg(il, th, 1, 1)
        return carry

    lax.fori_loop(0, ITERS, step, 0)
    out_ref[...] = basis[...]


def iterate(gram, start):
    order, rank = start.shape
    return pl.pallas_call(
        iteration_kernel,
        out_shape=jax.ShapeDtypeStruct((order, rank), F32),
        in_specs=[pl.BlockSpec(memory_space=pltpu.VMEM)] * 2,
        out_specs=pl.BlockSpec(memory_space=pltpu.VMEM),
        scratch_shapes=[
            pltpu.VMEM((order, order), BF16),
            pltpu.VMEM((order, order), BF16),
            pltpu.VMEM((rank, 2 * rank), F32),
            pltpu.VMEM((order, rank), F32),
        ],
        compiler_params=pltpu.CompilerParams(vmem_limit_bytes=48 << 20),
    )(gram, start)


def body(field, start_basis):
    rows_x, cells_y, cells_z = field.shape
    flat = field.reshape(rows_x, cells_y * cells_z)
    fibres = lax.all_to_all(flat, "gx", split_axis=1, concat_axis=0, tiled=True)
    partial_gram = jnp.dot(fibres, fibres.T, precision=lax.Precision.HIGH, preferred_element_type=F32)
    gram = lax.psum(partial_gram, ("gx", "gy", "gz"))
    basis = iterate(gram, start_basis)
    own_rows = lax.dynamic_slice_in_dim(basis, lax.axis_index("gx") * rows_x, rows_x, 0)
    scaled_basis = own_rows * jnp.sqrt(jnp.float32(basis.shape[0]))
    core_cols = jnp.dot(basis.T, fibres, precision=lax.Precision.HIGH, preferred_element_type=F32)
    core = lax.all_to_all(core_cols, "gx", split_axis=0, concat_axis=1, tiled=True)
    return (scaled_basis, core.reshape(core.shape[0], cells_y, cells_z))


def solution(mesh):
    placed = (P("gx", "gy", "gz"), P())
    return jax.shard_map(
        body,
        mesh=mesh,
        in_specs=placed,
        out_specs=(P("gx", None), P("gx", "gy", "gz")),
        check_vma=False,
    )
```

```python
import functools

import jax
import jax.numpy as jnp
from jax import lax
from jax.experimental import pallas as pl
from jax.experimental.pallas import tpu as pltpu
from jax.sharding import PartitionSpec as P

ITERS = 8
MESH = pl.DeviceIdType.MESH
F32 = jnp.float32
BF16 = jnp.bfloat16


def split(x):
    high = x.astype(BF16)
    return high, (x - high.astype(F32)).astype(BF16)


def dg(a, b, ca, cb):
    return lax.dot_general(a, b, (((ca,), (cb,)), ((), ())), preferred_element_type=F32)


def lower_inverse(aug, panel=8):
    n = aug.shape[0]
    row = lax.broadcasted_iota(jnp.int32, (panel, n), 0)
    for first in range(0, n, panel):
        left, right = aug[first : first + panel, :n], aug[first : first + panel, n:]
        cols = [jnp.broadcast_to(left[:, first + k : first + k + 1], (panel, n)) for k in range(panel)]
        pivots = None
        for i in range(panel):
            pivot = jnp.broadcast_to(cols[i][i : i + 1, :], (panel, n))
            ratio = jnp.where(row > i, cols[i], 0.0) * (1.0 / pivot)
            for k in range(i + 1, panel):
                cols[k] = cols[k] - ratio * jnp.broadcast_to(cols[k][i : i + 1, :], (panel, n))
            left = left - ratio * jnp.broadcast_to(left[i : i + 1, :], (panel, n))
            right = right - ratio * jnp.broadcast_to(right[i : i + 1, :], (panel, n))
            pivots = pivot if pivots is None else jnp.where(row == i, pivot, pivots)
        scale = lax.rsqrt(pivots)
        left, right = left * scale, right * scale
        aug[first : first + panel, n:] = right
        if first + panel < n:
            update = lax.dot_general(
                left,
                jnp.concatenate([left, right], axis=1),
                (((0,), (0,)), ((), ())),
                precision=lax.Precision.HIGHEST,
                preferred_element_type=F32,
            )
            aug[first + panel :, :] = aug[first + panel :, :] - update[first + panel :, :]


class Place:
    def __init__(self):
        gx, gy = lax.axis_index("gx"), lax.axis_index("gy")
        self.gx, self.gy = gx, gy
        self.core = gy % 2
        self.at = {"x": (gx % 2) * 2 + gy // 2, "y": gx // 2, "z": lax.axis_index("gz")}

    def along(self, axis, step):
        to = (self.at[axis] + step) % 4
        if axis == "z":
            return {"gz": to}
        if axis == "y":
            return {"gx": to * 2 + self.gx % 2}
        return {"gx": self.at["y"] * 2 + to // 2, "gy": (to % 2) * 2 + self.core}

    def partner(self):
        return {"gy": self.gy - self.core + 1 - self.core}


def greet(peers):
    barrier = pltpu.get_barrier_semaphore()
    for peer in peers:
        pl.semaphore_signal(barrier, inc=1, device_id=peer, device_id_type=MESH)
    pl.semaphore_wait(barrier, len(peers))


def push(src, dst, sems, k, peer):
    copy = pltpu.make_async_remote_copy(
        src_ref=src, dst_ref=dst, send_sem=sems.at[0, k], recv_sem=sems.at[1, k], device_id=peer, device_id_type=MESH
    )
    copy.start()
    return copy


STREAMS = (("z", "y", "x"), ("y", "x", "z"), ("x", "z", "y"))
HALF, THIRD, PIECE, BIT = 2304, 768, 192, 48
A2A_ORDER = (1, 2, 6, 4, 5, 3, 7)


def first_row(i, j):
    return (i * (i + 1) // 2 + j) * 128


def gather_products(me, field, part, land, fh, fl, sems):
    own = pltpu.make_async_copy(field.at[:, pl.ds(8 * me, 8), :], land.at[0], sems.at[0, 0])
    own.start()
    copies = {}
    for d in A2A_ORDER:
        peer = me ^ d
        copies[d] = push(field.at[:, pl.ds(8 * peer, 8), :], land.at[d], sems, d, {"gx": peer})

    def halves(d):
        rows = pl.ds(pl.multiple_of((me ^ d) * 128, 128), 128)
        for a in range(8):
            high, low = split(land[d, :, a, :])
            fh[rows, 128 * a : 128 * a + 128] = high
            fl[rows, 128 * a : 128 * a + 128] = low

    own.wait()
    halves(0)
    for d in A2A_ORDER:
        copies[d].wait_recv()
        halves(d)
    for panel in range(4):
        c = 256 * panel
        bh, bl = fh[c : c + 256, :], fl[c : c + 256, :]
        ah, al = fh[c:, :], fl[c:, :]
        block = dg(ah, bh, 1, 1) + dg(ah, bl, 1, 1) + dg(al, bh, 1, 1)
        for j in (2 * panel, 2 * panel + 1):
            for i in range(j, 8):
                top = first_row(i, j)
                part[top : top + 128, :] = block[128 * i - c : 128 * i - c + 128, 128 * j - c : 128 * j - c + 128]
    for d in A2A_ORDER:
        copies[d].wait_send()


def reduce_all(place, part, full, land0, land1, land2, land3, sems):
    core = place.core
    mine = core * HALF
    pending = []

    def send(src, dst, k, peer):
        copy = push(src, dst, sems, k, peer)
        pending.append(copy)
        return copy

    def rows(ref, start, size):
        return ref.at[pl.ds(pl.multiple_of(start, 16), size), :]

    def bases(s):
        a, b, _ = (place.at[axis] for axis in STREAMS[s])
        top = mine + THIRD * s
        return top, top + PIECE * a, top + PIECE * a + BIT * b

    def add(start, size, terms):
        where = pl.ds(pl.multiple_of(start, 16), size)
        part[where, :] = part[where, :] + terms

    k = 0
    swap, first, second, third, back, again, last = [], {}, {}, {}, {}, {}, []
    for s in range(3):
        other = (1 - core) * HALF + THIRD * s
        swap.append(send(rows(part, other, THIRD), rows(land0, THIRD * s, THIRD), k, place.partner()))
        k += 1
    for s in range(3):
        swap[s].wait_recv()
        top, _, _ = bases(s)
        add(top, THIRD, land0[THIRD * s : THIRD * s + THIRD, :])
        axis = STREAMS[s][0]
        for e in (2, 1, 3):
            to = (place.at[axis] + e) % 4
            slot = (3 * s + 3 - e) * PIECE
            first[s, e] = send(rows(part, top + PIECE * to, PIECE), rows(land1, slot, PIECE), k, place.along(axis, e))
            k += 1
    for s in range(3):
        for e in (2, 1, 3):
            first[s, e].wait_recv()
        _, mid, _ = bases(s)
        got = [land1[(3 * s + t) * PIECE : (3 * s + t + 1) * PIECE, :] for t in range(3)]
        add(mid, PIECE, got[0] + got[1] + got[2])
        axis = STREAMS[s][1]
        for e in (2, 1, 3):
            to = (place.at[axis] + e) % 4
            slot = (3 * s + 3 - e) * BIT
            second[s, e] = send(rows(part, mid + BIT * to, BIT), rows(land2, slot, BIT), k, place.along(axis, e))
            k += 1
    for s in range(3):
        for e in (2, 1, 3):
            second[s, e].wait_recv()
        _, _, low = bases(s)
        got = [land2[(3 * s + t) * BIT : (3 * s + t + 1) * BIT, :] for t in range(3)]
        add(low, BIT, got[0] + got[1] + got[2])
        axis = STREAMS[s][2]
        for e in (2, 1, 3):
            slot = (3 * s + 3 - e) * BIT
            third[s, e] = send(rows(part, low, BIT), rows(land3, slot, BIT), k, place.along(axis, e))
            k += 1
    for s in range(3):
        for e in (2, 1, 3):
            third[s, e].wait_recv()
        _, _, low = bases(s)
        got = [land3[(3 * s + t) * BIT : (3 * s + t + 1) * BIT, :] for t in range(3)]
        even = place.at[STREAMS[s][2]] % 2 == 0
        where = pl.ds(pl.multiple_of(low, 16), BIT)
        near = jnp.where(even, got[0], got[2])
        far = jnp.where(even, got[2], got[0])
        full[where, :] = (part[where, :] + near) + (got[1] + far)
        axis = STREAMS[s][1]
        for e in (2, 1, 3):
            back[s, e] = send(rows(full, low, BIT), rows(full, low, BIT), k, place.along(axis, e))
            k += 1
    for s in range(3):
        for e in (2, 1, 3):
            back[s, e].wait_recv()
        _, mid, _ = bases(s)
        axis = STREAMS[s][0]
        for e in (2, 1, 3):
            again[s, e] = send(rows(full, mid, PIECE), rows(full, mid, PIECE), k, place.along(axis, e))
            k += 1
        last.append(send(rows(full, mid, PIECE), rows(full, mid, PIECE), k, place.partner()))
        k += 1
    for s in range(3):
        top, _, _ = bases(s)
        for e in (1, 3, 2):
            again[s, e].wait_recv()

            came = (place.at[STREAMS[s][0]] + 4 - e) % 4
            piece = top + PIECE * came
            last.append(send(rows(full, piece, PIECE), rows(full, piece, PIECE), k, place.partner()))
            k += 1
    for copy in last:
        copy.wait_recv()
    for copy in pending:
        copy.wait_send()


N_COPIES = 3 + 9 * 3 + 9 + 12 + 9


def gram_kernel(field, full, fh_out, fl_out, land, fh, fl, part, land0, land1, land2, land3, sems, more, keep):
    place = Place()
    me = place.gx
    peers = [{"gx": me ^ d} for d in range(1, 8)] + [place.partner()]
    peers += [place.along("z", e) for e in (1, 2, 3)] + [place.along("x", e) for e in (1, 3)]
    greet(peers)
    gather_products(me, field, part, land, fh, fl, sems)
    out = [pltpu.make_async_copy(fh, fh_out, keep.at[0]), pltpu.make_async_copy(fl, fl_out, keep.at[1])]
    for copy in out:
        copy.start()
    reduce_all(place, part, full, land0, land1, land2, land3, more)
    for copy in out:
        copy.wait()


def gram_of(field):
    rows, order = field.shape[0], 1024
    hbm, vmem = pl.BlockSpec(memory_space=pl.ANY), pl.BlockSpec(memory_space=pltpu.VMEM)
    kept = jax.ShapeDtypeStruct((order, order), BF16)
    return pl.pallas_call(
        gram_kernel,
        out_shape=(jax.ShapeDtypeStruct((2 * HALF, 128), F32), kept, kept),
        in_specs=[hbm],
        out_specs=(vmem, hbm, hbm),
        scratch_shapes=[
            pltpu.VMEM((8, rows, 8, 128), F32),
            pltpu.VMEM((order, order), BF16),
            pltpu.VMEM((order, order), BF16),
            pltpu.VMEM((2 * HALF, 128), F32),
            pltpu.VMEM((HALF, 128), F32),
            pltpu.VMEM((9 * PIECE, 128), F32),
            pltpu.VMEM((9 * BIT, 128), F32),
            pltpu.VMEM((9 * BIT, 128), F32),
            pltpu.SemaphoreType.DMA((2, 8)),
            pltpu.SemaphoreType.DMA((2, N_COPIES)),
            pltpu.SemaphoreType.DMA((2,)),
        ],
        compiler_params=pltpu.CompilerParams(collective_id=0, has_side_effects=True, vmem_limit_bytes=56 << 20),
    )(field)


def iteration_kernel(gram_ref, start_ref, out_ref, gram_high, gram_low, aug, basis):
    for i in range(8):
        for j in range(i + 1):
            block = gram_ref[first_row(i, j) : first_row(i, j) + 128, :]
            places = [(i, j, block)] if i == j else [(i, j, block), (j, i, block.T)]
            for r, c, value in places:
                where = (slice(128 * r, 128 * r + 128), slice(128 * c, 128 * c + 128))
                gram_high[where], gram_low[where] = split(value)
    basis[...] = start_ref[...]
    n = aug.shape[0]
    shape = (n, n)
    eye = (lax.broadcasted_iota(jnp.int32, shape, 0) == lax.broadcasted_iota(jnp.int32, shape, 1)).astype(F32)

    def step(_, carry):
        bh, bl = split(basis[...])
        both = dg(gram_high[...], jnp.concatenate([bh, bl], axis=1), 1, 0)
        image = both[:, :n] + both[:, n:] + dg(gram_low[...], bh, 1, 0)
        ih, il = split(image)
        both = dg(ih, jnp.concatenate([ih, il], axis=1), 0, 0)
        mixed = both[:, n:]
        aug[:, :n] = both[:, :n] + mixed + mixed.T
        aug[:, n:] = eye
        lower_inverse(aug)
        th, tl = split(aug[:, n:])
        both = dg(ih, jnp.concatenate([th, tl], axis=0), 1, 1)
        basis[...] = both[:, :n] + both[:, n:] + dg(il, th, 1, 1)
        return carry

    lax.fori_loop(0, ITERS, step, 0)
    out_ref[...] = basis[...]


def iterate(gram, start):
    order, rank = start.shape
    return pl.pallas_call(
        iteration_kernel,
        out_shape=jax.ShapeDtypeStruct((order, rank), F32),
        in_specs=[pl.BlockSpec(memory_space=pltpu.VMEM)] * 2,
        out_specs=pl.BlockSpec(memory_space=pltpu.VMEM),
        scratch_shapes=[
            pltpu.VMEM((order, order), BF16),
            pltpu.VMEM((order, order), BF16),
            pltpu.VMEM((rank, 2 * rank), F32),
            pltpu.VMEM((order, rank), F32),
        ],
        compiler_params=pltpu.CompilerParams(vmem_limit_bytes=48 << 20),
    )(gram, start)


def core_kernel(basis_ref, fh, fl, core, scaled, cols, sems):
    me = lax.axis_index("gx")
    greet([{"gx": me ^ d} for d in range(1, 8)])
    high, low = split(basis_ref[...])
    flat = cols.reshape(1024, 128)
    for a in range(0, 8, 2):
        c = slice(128 * a, 128 * a + 256)
        part = dg(high, fh[:, c], 0, 0) + dg(high, fl[:, c], 0, 0) + dg(low, fh[:, c], 0, 0)
        flat[pl.ds(a, 128, stride=8), :] = part[:, :128]
        flat[pl.ds(a + 1, 128, stride=8), :] = part[:, 128:]
    copies = []
    here = pl.ds(pl.multiple_of(8 * me, 8), 8)
    for d in A2A_ORDER:
        peer = me ^ d
        copies.append(push(cols.at[pl.ds(16 * peer, 16)], core.at[:, here, :], sems, d, {"gx": peer}))
    own = pltpu.make_async_copy(cols.at[pl.ds(16 * me, 16)], core.at[:, here, :], sems.at[0, 0])
    own.start()
    scaled[...] = basis_ref[pl.ds(pl.multiple_of(128 * me, 128), 128), :] * jnp.sqrt(F32(1024))
    own.wait()
    for copy in copies:
        copy.wait()


def core_of(basis, fh, fl):
    vmem = pl.BlockSpec(memory_space=pltpu.VMEM)
    return pl.pallas_call(
        core_kernel,
        out_shape=(jax.ShapeDtypeStruct((16, 64, 128), F32), jax.ShapeDtypeStruct((128, 128), F32)),
        in_specs=[vmem] * 3,
        out_specs=(vmem, vmem),
        scratch_shapes=[pltpu.VMEM((128, 8, 128), F32), pltpu.SemaphoreType.DMA((2, 8))],
        compiler_params=pltpu.CompilerParams(collective_id=1, has_side_effects=True, vmem_limit_bytes=40 << 20),
    )(basis, fh, fl)


def body(field, start_basis):
    gram, fh, fl = gram_of(field)
    basis = iterate(gram, start_basis)
    core, scaled_basis = core_of(basis, fh, fl)
    return (scaled_basis, core)


def solution(mesh):
    placed = (P("gx", "gy", "gz"), P())
    return jax.shard_map(
        body,
        mesh=mesh,
        in_specs=placed,
        out_specs=(P("gx", None), P("gx", "gy", "gz")),
        check_vma=False,
    )
```

```python
import functools

import jax
import jax.numpy as jnp
from jax import lax
from jax.experimental import pallas as pl
from jax.experimental.pallas import tpu as pltpu
from jax.sharding import PartitionSpec as P

ITERS = 8
MESH = pl.DeviceIdType.MESH
F32 = jnp.float32
BF16 = jnp.bfloat16


def split(x):
    high = x.astype(BF16)
    return high, (x - high.astype(F32)).astype(BF16)


def dg(a, b, ca, cb):
    return lax.dot_general(a, b, (((ca,), (cb,)), ((), ())), preferred_element_type=F32)


def split3(x):
    high = x.astype(BF16)
    rest = x - high.astype(F32)
    mid = rest.astype(BF16)
    return high, mid, (rest - mid.astype(F32)).astype(BF16)


def lower_inverse(aug, panel=16):
    n = aug.shape[0]
    row = lax.broadcasted_iota(jnp.int32, (panel, n), 0)
    for first in range(0, n, panel):
        left, right = aug[first : first + panel, :n], aug[first : first + panel, n:]
        cols = [jnp.broadcast_to(left[:, first + k : first + k + 1], (panel, n)) for k in range(panel)]
        pivots = None
        for i in range(panel):
            pivot = jnp.broadcast_to(cols[i][i : i + 1, :], (panel, n))
            ratio = jnp.where(row > i, cols[i], 0.0) * (1.0 / pivot)
            for k in range(i + 1, panel):
                cols[k] = cols[k] - ratio * jnp.broadcast_to(cols[k][i : i + 1, :], (panel, n))
            left = left - ratio * jnp.broadcast_to(left[i : i + 1, :], (panel, n))
            right = right - ratio * jnp.broadcast_to(right[i : i + 1, :], (panel, n))
            pivots = pivot if pivots is None else jnp.where(row == i, pivot, pivots)
        scale = lax.rsqrt(pivots)
        left, right = left * scale, right * scale
        aug[first : first + panel, n:] = right
        if first + panel < n:
            high, mid, low = split3(jnp.concatenate([left, right], axis=1))
            a = jnp.concatenate([part[:, :n] for part in (high, high, mid, high, low, mid)], axis=0)
            b = jnp.concatenate([high, mid, high, low, high, mid], axis=0)
            update = dg(a, b, 0, 0)
            aug[first + panel :, :] = aug[first + panel :, :] - update[first + panel :, :]


class Place:
    def __init__(self):
        gx, gy = lax.axis_index("gx"), lax.axis_index("gy")
        self.gx, self.gy = gx, gy
        self.core = gy % 2
        self.at = {"x": (gx % 2) * 2 + gy // 2, "y": gx // 2, "z": lax.axis_index("gz")}

    def along(self, axis, step):
        to = (self.at[axis] + step) % 4
        if axis == "z":
            return {"gz": to}
        if axis == "y":
            return {"gx": to * 2 + self.gx % 2}
        return {"gx": self.at["y"] * 2 + to // 2, "gy": (to % 2) * 2 + self.core}

    def partner(self):
        return {"gy": self.gy - self.core + 1 - self.core}


def greet(peers):
    barrier = pltpu.get_barrier_semaphore()
    for peer in peers:
        pl.semaphore_signal(barrier, inc=1, device_id=peer, device_id_type=MESH)
    pl.semaphore_wait(barrier, len(peers))


def push(src, dst, sems, k, peer):
    copy = pltpu.make_async_remote_copy(
        src_ref=src, dst_ref=dst, send_sem=sems.at[0, k], recv_sem=sems.at[1, k], device_id=peer, device_id_type=MESH
    )
    copy.start()
    return copy


STREAMS = (("z", "y", "x"), ("y", "x", "z"), ("x", "z", "y"))
HALF, THIRD, PIECE, BIT = 2304, 768, 192, 48
A2A_ORDER = (1, 2, 6, 4, 5, 3, 7)


def first_row(i, j):
    return (i * (i + 1) // 2 + j) * 128


def gather_products(me, field, part, land, fh, fl, sems):
    own = pltpu.make_async_copy(field.at[:, pl.ds(8 * me, 8), :], land.at[0], sems.at[0, 0])
    own.start()
    copies = {}
    for d in A2A_ORDER:
        peer = me ^ d
        copies[d] = push(field.at[:, pl.ds(8 * peer, 8), :], land.at[d], sems, d, {"gx": peer})

    def halves(d):
        rows = pl.ds(pl.multiple_of((me ^ d) * 128, 128), 128)
        for a in range(8):
            high, low = split(land[d, :, a, :])
            fh[rows, 128 * a : 128 * a + 128] = high
            fl[rows, 128 * a : 128 * a + 128] = low

    own.wait()
    halves(0)
    for d in A2A_ORDER:
        copies[d].wait_recv()
        halves(d)
    for panel in range(4):
        c = 256 * panel
        bh, bl = fh[c : c + 256, :], fl[c : c + 256, :]
        ah, al = fh[c:, :], fl[c:, :]
        block = dg(ah, bh, 1, 1) + dg(ah, bl, 1, 1) + dg(al, bh, 1, 1)
        for j in (2 * panel, 2 * panel + 1):
            for i in range(j, 8):
                top = first_row(i, j)
                part[top : top + 128, :] = block[128 * i - c : 128 * i - c + 128, 128 * j - c : 128 * j - c + 128]
    for d in A2A_ORDER:
        copies[d].wait_send()


def reduce_all(place, part, full, land0, land1, land2, land3, sems):
    core = place.core
    mine = core * HALF
    pending = []

    def send(src, dst, k, peer):
        copy = push(src, dst, sems, k, peer)
        pending.append(copy)
        return copy

    def rows(ref, start, size):
        return ref.at[pl.ds(pl.multiple_of(start, 16), size), :]

    def bases(s):
        a, b, _ = (place.at[axis] for axis in STREAMS[s])
        top = mine + THIRD * s
        return top, top + PIECE * a, top + PIECE * a + BIT * b

    def add(start, size, terms):
        where = pl.ds(pl.multiple_of(start, 16), size)
        part[where, :] = part[where, :] + terms

    k = 0
    swap, first, second, third, back, again, last = [], {}, {}, {}, {}, {}, []
    for s in range(3):
        other = (1 - core) * HALF + THIRD * s
        swap.append(send(rows(part, other, THIRD), rows(land0, THIRD * s, THIRD), k, place.partner()))
        k += 1
    for s in range(3):
        swap[s].wait_recv()
        top, _, _ = bases(s)
        add(top, THIRD, land0[THIRD * s : THIRD * s + THIRD, :])
        axis = STREAMS[s][0]
        for e in (2, 1, 3):
            to = (place.at[axis] + e) % 4
            slot = (3 * s + 3 - e) * PIECE
            first[s, e] = send(rows(part, top + PIECE * to, PIECE), rows(land1, slot, PIECE), k, place.along(axis, e))
            k += 1
    for s in range(3):
        for e in (2, 1, 3):
            first[s, e].wait_recv()
        _, mid, _ = bases(s)
        got = [land1[(3 * s + t) * PIECE : (3 * s + t + 1) * PIECE, :] for t in range(3)]
        add(mid, PIECE, got[0] + got[1] + got[2])
        axis = STREAMS[s][1]
        for e in (2, 1, 3):
            to = (place.at[axis] + e) % 4
            slot = (3 * s + 3 - e) * BIT
            second[s, e] = send(rows(part, mid + BIT * to, BIT), rows(land2, slot, BIT), k, place.along(axis, e))
            k += 1
    for s in range(3):
        for e in (2, 1, 3):
            second[s, e].wait_recv()
        _, _, low = bases(s)
        got = [land2[(3 * s + t) * BIT : (3 * s + t + 1) * BIT, :] for t in range(3)]
        add(low, BIT, got[0] + got[1] + got[2])
        axis = STREAMS[s][2]
        for e in (2, 1, 3):
            slot = (3 * s + 3 - e) * BIT
            third[s, e] = send(rows(part, low, BIT), rows(land3, slot, BIT), k, place.along(axis, e))
            k += 1
    for s in range(3):
        for e in (2, 1, 3):
            third[s, e].wait_recv()
        _, _, low = bases(s)
        got = [land3[(3 * s + t) * BIT : (3 * s + t + 1) * BIT, :] for t in range(3)]
        even = place.at[STREAMS[s][2]] % 2 == 0
        where = pl.ds(pl.multiple_of(low, 16), BIT)
        near = jnp.where(even, got[0], got[2])
        far = jnp.where(even, got[2], got[0])
        full[where, :] = (part[where, :] + near) + (got[1] + far)
        axis = STREAMS[s][1]
        for e in (2, 1, 3):
            back[s, e] = send(rows(full, low, BIT), rows(full, low, BIT), k, place.along(axis, e))
            k += 1
    for s in range(3):
        for e in (2, 1, 3):
            back[s, e].wait_recv()
        _, mid, _ = bases(s)
        axis = STREAMS[s][0]
        for e in (2, 1, 3):
            again[s, e] = send(rows(full, mid, PIECE), rows(full, mid, PIECE), k, place.along(axis, e))
            k += 1
        last.append(send(rows(full, mid, PIECE), rows(full, mid, PIECE), k, place.partner()))
        k += 1
    for s in range(3):
        top, _, _ = bases(s)
        for e in (1, 3, 2):
            again[s, e].wait_recv()

            came = (place.at[STREAMS[s][0]] + 4 - e) % 4
            piece = top + PIECE * came
            last.append(send(rows(full, piece, PIECE), rows(full, piece, PIECE), k, place.partner()))
            k += 1
    for copy in last:
        copy.wait_recv()
    for copy in pending:
        copy.wait_send()


N_COPIES = 3 + 9 * 3 + 9 + 12 + 9


def gram_kernel(field, full, fh_out, fl_out, land, fh, fl, part, land0, land1, land2, land3, sems, more, keep):
    place = Place()
    me = place.gx
    peers = [{"gx": me ^ d} for d in range(1, 8)] + [place.partner()]
    peers += [place.along("z", e) for e in (1, 2, 3)] + [place.along("x", e) for e in (1, 3)]
    greet(peers)
    gather_products(me, field, part, land, fh, fl, sems)
    out = [pltpu.make_async_copy(fh, fh_out, keep.at[0]), pltpu.make_async_copy(fl, fl_out, keep.at[1])]
    for copy in out:
        copy.start()
    reduce_all(place, part, full, land0, land1, land2, land3, more)
    for copy in out:
        copy.wait()


def gram_of(field):
    rows, order = field.shape[0], 1024
    hbm, vmem = pl.BlockSpec(memory_space=pl.ANY), pl.BlockSpec(memory_space=pltpu.VMEM)
    kept = jax.ShapeDtypeStruct((order, order), BF16)
    return pl.pallas_call(
        gram_kernel,
        out_shape=(jax.ShapeDtypeStruct((2 * HALF, 128), F32), kept, kept),
        in_specs=[hbm],
        out_specs=(vmem, hbm, hbm),
        scratch_shapes=[
            pltpu.VMEM((8, rows, 8, 128), F32),
            pltpu.VMEM((order, order), BF16),
            pltpu.VMEM((order, order), BF16),
            pltpu.VMEM((2 * HALF, 128), F32),
            pltpu.VMEM((HALF, 128), F32),
            pltpu.VMEM((9 * PIECE, 128), F32),
            pltpu.VMEM((9 * BIT, 128), F32),
            pltpu.VMEM((9 * BIT, 128), F32),
            pltpu.SemaphoreType.DMA((2, 8)),
            pltpu.SemaphoreType.DMA((2, N_COPIES)),
            pltpu.SemaphoreType.DMA((2,)),
        ],
        compiler_params=pltpu.CompilerParams(collective_id=0, has_side_effects=True, vmem_limit_bytes=56 << 20),
    )(field)


def iteration_kernel(gram_ref, start_ref, out_ref, gram_high, gram_low, aug, basis):
    for i in range(8):
        for j in range(i + 1):
            block = gram_ref[first_row(i, j) : first_row(i, j) + 128, :]
            places = [(i, j, block)] if i == j else [(i, j, block), (j, i, block.T)]
            for r, c, value in places:
                where = (slice(128 * r, 128 * r + 128), slice(128 * c, 128 * c + 128))
                gram_high[where], gram_low[where] = split(value)
    basis[...] = start_ref[...]
    n = aug.shape[0]
    shape = (n, n)
    eye = (lax.broadcasted_iota(jnp.int32, shape, 0) == lax.broadcasted_iota(jnp.int32, shape, 1)).astype(F32)

    def step(_, carry):
        bh, bl = split(basis[...])
        both = dg(gram_high[...], jnp.concatenate([bh, bl], axis=1), 1, 0)
        image = both[:, :n] + both[:, n:] + dg(gram_low[...], bh, 1, 0)
        ih, il = split(image)
        both = dg(ih, jnp.concatenate([ih, il], axis=1), 0, 0)
        mixed = both[:, n:]
        aug[:, :n] = both[:, :n] + mixed + mixed.T
        aug[:, n:] = eye
        lower_inverse(aug)
        th, tl = split(aug[:, n:])
        both = dg(ih, jnp.concatenate([th, tl], axis=0), 1, 1)
        basis[...] = both[:, :n] + both[:, n:] + dg(il, th, 1, 1)
        return carry

    lax.fori_loop(0, ITERS, step, 0)
    out_ref[...] = basis[...]


def iterate(gram, start):
    order, rank = start.shape
    return pl.pallas_call(
        iteration_kernel,
        out_shape=jax.ShapeDtypeStruct((order, rank), F32),
        in_specs=[pl.BlockSpec(memory_space=pltpu.VMEM)] * 2,
        out_specs=pl.BlockSpec(memory_space=pltpu.VMEM),
        scratch_shapes=[
            pltpu.VMEM((order, order), BF16),
            pltpu.VMEM((order, order), BF16),
            pltpu.VMEM((rank, 2 * rank), F32),
            pltpu.VMEM((order, rank), F32),
        ],
        compiler_params=pltpu.CompilerParams(vmem_limit_bytes=48 << 20),
    )(gram, start)


def core_kernel(basis_ref, fh, fl, core, scaled, cols, sems):
    me = lax.axis_index("gx")
    greet([{"gx": me ^ d} for d in range(1, 8)])
    high, low = split(basis_ref[...])
    flat = cols.reshape(1024, 128)
    for a in range(0, 8, 2):
        c = slice(128 * a, 128 * a + 256)
        part = dg(high, fh[:, c], 0, 0) + dg(high, fl[:, c], 0, 0) + dg(low, fh[:, c], 0, 0)
        flat[pl.ds(a, 128, stride=8), :] = part[:, :128]
        flat[pl.ds(a + 1, 128, stride=8), :] = part[:, 128:]
    copies = []
    here = pl.ds(pl.multiple_of(8 * me, 8), 8)
    for d in A2A_ORDER:
        peer = me ^ d
        copies.append(push(cols.at[pl.ds(16 * peer, 16)], core.at[:, here, :], sems, d, {"gx": peer}))
    own = pltpu.make_async_copy(cols.at[pl.ds(16 * me, 16)], core.at[:, here, :], sems.at[0, 0])
    own.start()
    scaled[...] = basis_ref[pl.ds(pl.multiple_of(128 * me, 128), 128), :] * jnp.sqrt(F32(1024))
    own.wait()
    for copy in copies:
        copy.wait()


def core_of(basis, fh, fl):
    vmem = pl.BlockSpec(memory_space=pltpu.VMEM)
    return pl.pallas_call(
        core_kernel,
        out_shape=(jax.ShapeDtypeStruct((16, 64, 128), F32), jax.ShapeDtypeStruct((128, 128), F32)),
        in_specs=[vmem] * 3,
        out_specs=(vmem, vmem),
        scratch_shapes=[pltpu.VMEM((128, 8, 128), F32), pltpu.SemaphoreType.DMA((2, 8))],
        compiler_params=pltpu.CompilerParams(collective_id=1, has_side_effects=True, vmem_limit_bytes=40 << 20),
    )(basis, fh, fl)


def body(field, start_basis):
    gram, fh, fl = gram_of(field)
    basis = iterate(gram, start_basis)
    core, scaled_basis = core_of(basis, fh, fl)
    return (scaled_basis, core)


def solution(mesh):
    placed = (P("gx", "gy", "gz"), P())
    return jax.shard_map(
        body,
        mesh=mesh,
        in_specs=placed,
        out_specs=(P("gx", None), P("gx", "gy", "gz")),
        check_vma=False,
    )
```

```python
import functools

import jax
import jax.numpy as jnp
from jax import lax
from jax.experimental import pallas as pl
from jax.experimental.pallas import tpu as pltpu
from jax.sharding import PartitionSpec as P

ITERS = 8
MESH = pl.DeviceIdType.MESH
F32 = jnp.float32
BF16 = jnp.bfloat16


def split(x):
    high = x.astype(BF16)
    return high, (x - high.astype(F32)).astype(BF16)


def dg(a, b, ca, cb):
    return lax.dot_general(a, b, (((ca,), (cb,)), ((), ())), preferred_element_type=F32)


def split3(x):
    high = x.astype(BF16)
    rest = x - high.astype(F32)
    mid = rest.astype(BF16)
    return high, mid, (rest - mid.astype(F32)).astype(BF16)


def lower_inverse(aug, panel=16):
    n = aug.shape[0]
    row = lax.broadcasted_iota(jnp.int32, (panel, n), 0)
    for first in range(0, n, panel):
        left, right = aug[first : first + panel, :n], aug[first : first + panel, n:]
        cols = [jnp.broadcast_to(left[:, first + k : first + k + 1], (panel, n)) for k in range(panel)]
        pivots = None
        for i in range(panel):
            pivot = jnp.broadcast_to(cols[i][i : i + 1, :], (panel, n))
            ratio = jnp.where(row > i, cols[i], 0.0) * (1.0 / pivot)
            for k in range(i + 1, panel):
                cols[k] = cols[k] - ratio * jnp.broadcast_to(cols[k][i : i + 1, :], (panel, n))
            left = left - ratio * jnp.broadcast_to(left[i : i + 1, :], (panel, n))
            right = right - ratio * jnp.broadcast_to(right[i : i + 1, :], (panel, n))
            pivots = pivot if pivots is None else jnp.where(row == i, pivot, pivots)
        scale = lax.rsqrt(pivots)
        left, right = left * scale, right * scale
        aug[first : first + panel, n:] = right
        if first + panel < n:
            high, mid, low = split3(jnp.concatenate([left, right], axis=1))
            a = jnp.concatenate([part[:, :n] for part in (high, high, mid, high, low, mid)], axis=0)
            b = jnp.concatenate([high, mid, high, low, high, mid], axis=0)
            update = dg(a, b, 0, 0)
            aug[first + panel :, :] = aug[first + panel :, :] - update[first + panel :, :]


class Place:
    def __init__(self):
        gx, gy = lax.axis_index("gx"), lax.axis_index("gy")
        self.gx, self.gy = gx, gy
        self.core = gy % 2
        self.at = {"x": (gx % 2) * 2 + gy // 2, "y": gx // 2, "z": lax.axis_index("gz")}

    def along(self, axis, step):
        to = (self.at[axis] + step) % 4
        if axis == "z":
            return {"gz": to}
        if axis == "y":
            return {"gx": to * 2 + self.gx % 2}
        return {"gx": self.at["y"] * 2 + to // 2, "gy": (to % 2) * 2 + self.core}

    def partner(self):
        return {"gy": self.gy - self.core + 1 - self.core}


def greet(peers):
    barrier = pltpu.get_barrier_semaphore()
    for peer in peers:
        pl.semaphore_signal(barrier, inc=1, device_id=peer, device_id_type=MESH)
    pl.semaphore_wait(barrier, len(peers))


def push(src, dst, sems, k, peer):
    copy = pltpu.make_async_remote_copy(
        src_ref=src, dst_ref=dst, send_sem=sems.at[0, k], recv_sem=sems.at[1, k], device_id=peer, device_id_type=MESH
    )
    copy.start()
    return copy


STREAMS = (("z", "y", "x"), ("y", "x", "z"), ("x", "z", "y"))
HALF, THIRD, PIECE, BIT = 2304, 768, 192, 48
A2A_ORDER = (1, 2, 6, 4, 5, 3, 7)
ARRIVAL = (0,) + A2A_ORDER


def first_row(i, j):
    return (i * (i + 1) // 2 + j) * 128


def row_block(k):
    return pl.ds(pl.multiple_of(k * 128, 128), 128)


def gather_products(me, field, part, land, fh, fl, sems):
    own = pltpu.make_async_copy(field.at[:, pl.ds(8 * me, 8), :], land.at[0], sems.at[0, 0])
    own.start()
    copies = {}
    for d in A2A_ORDER:
        peer = me ^ d
        copies[d] = push(field.at[:, pl.ds(8 * peer, 8), :], land.at[d], sems, d, {"gx": peer})
    for s, d in enumerate(ARRIVAL):
        if d == 0:
            own.wait()
        else:
            copies[d].wait_recv()
        here = slice(128 * s, 128 * s + 128)
        for a in range(8):
            high, low = split(land[d, :, a, :])
            fh[here, 128 * a : 128 * a + 128] = high
            fl[here, 128 * a : 128 * a + 128] = low
        upto = slice(0, 128 * s + 128)
        both = dg(fh[upto, :], jnp.concatenate([fh[here, :], fl[here, :]], axis=0), 1, 1)
        block = both[:, :128] + both[:, 128:] + dg(fl[upto, :], fh[here, :], 1, 1)
        j = me ^ d
        for t in range(s + 1):
            i = me ^ ARRIVAL[t]
            value = block[128 * t : 128 * t + 128, :]
            if t < s:
                value = jnp.where(i > j, value, value.T)
            top = first_row(jnp.maximum(i, j), jnp.minimum(i, j))
            part[pl.ds(pl.multiple_of(top, 128), 128), :] = value
    for d in A2A_ORDER:
        copies[d].wait_send()


def reduce_all(place, part, full, land0, land1, land2, land3, sems):
    core = place.core
    mine = core * HALF
    pending = []

    def send(src, dst, k, peer):
        copy = push(src, dst, sems, k, peer)
        pending.append(copy)
        return copy

    def rows(ref, start, size):
        return ref.at[pl.ds(pl.multiple_of(start, 16), size), :]

    def bases(s):
        a, b, _ = (place.at[axis] for axis in STREAMS[s])
        top = mine + THIRD * s
        return top, top + PIECE * a, top + PIECE * a + BIT * b

    def add(start, size, terms):
        where = pl.ds(pl.multiple_of(start, 16), size)
        part[where, :] = part[where, :] + terms

    k = 0
    swap, first, second, third, back, again, last = [], {}, {}, {}, {}, {}, []
    for s in range(3):
        other = (1 - core) * HALF + THIRD * s
        swap.append(send(rows(part, other, THIRD), rows(land0, THIRD * s, THIRD), k, place.partner()))
        k += 1
    for s in range(3):
        swap[s].wait_recv()
        top, _, _ = bases(s)
        add(top, THIRD, land0[THIRD * s : THIRD * s + THIRD, :])
        axis = STREAMS[s][0]
        for e in (2, 1, 3):
            to = (place.at[axis] + e) % 4
            slot = (3 * s + 3 - e) * PIECE
            first[s, e] = send(rows(part, top + PIECE * to, PIECE), rows(land1, slot, PIECE), k, place.along(axis, e))
            k += 1
    for s in range(3):
        for e in (2, 1, 3):
            first[s, e].wait_recv()
        _, mid, _ = bases(s)
        got = [land1[(3 * s + t) * PIECE : (3 * s + t + 1) * PIECE, :] for t in range(3)]
        add(mid, PIECE, got[0] + got[1] + got[2])
        axis = STREAMS[s][1]
        for e in (2, 1, 3):
            to = (place.at[axis] + e) % 4
            slot = (3 * s + 3 - e) * BIT
            second[s, e] = send(rows(part, mid + BIT * to, BIT), rows(land2, slot, BIT), k, place.along(axis, e))
            k += 1
    for s in range(3):
        for e in (2, 1, 3):
            second[s, e].wait_recv()
        _, _, low = bases(s)
        got = [land2[(3 * s + t) * BIT : (3 * s + t + 1) * BIT, :] for t in range(3)]
        add(low, BIT, got[0] + got[1] + got[2])
        axis = STREAMS[s][2]
        for e in (2, 1, 3):
            slot = (3 * s + 3 - e) * BIT
            third[s, e] = send(rows(part, low, BIT), rows(land3, slot, BIT), k, place.along(axis, e))
            k += 1
    for s in range(3):
        for e in (2, 1, 3):
            third[s, e].wait_recv()
        _, _, low = bases(s)
        got = [land3[(3 * s + t) * BIT : (3 * s + t + 1) * BIT, :] for t in range(3)]
        even = place.at[STREAMS[s][2]] % 2 == 0
        where = pl.ds(pl.multiple_of(low, 16), BIT)
        near = jnp.where(even, got[0], got[2])
        far = jnp.where(even, got[2], got[0])
        full[where, :] = (part[where, :] + near) + (got[1] + far)
        axis = STREAMS[s][1]
        for e in (2, 1, 3):
            back[s, e] = send(rows(full, low, BIT), rows(full, low, BIT), k, place.along(axis, e))
            k += 1
    for s in range(3):
        for e in (2, 1, 3):
            back[s, e].wait_recv()
        _, mid, _ = bases(s)
        axis = STREAMS[s][0]
        for e in (2, 1, 3):
            again[s, e] = send(rows(full, mid, PIECE), rows(full, mid, PIECE), k, place.along(axis, e))
            k += 1
        last.append(send(rows(full, mid, PIECE), rows(full, mid, PIECE), k, place.partner()))
        k += 1
    for s in range(3):
        top, _, _ = bases(s)
        for e in (1, 3, 2):
            again[s, e].wait_recv()

            came = (place.at[STREAMS[s][0]] + 4 - e) % 4
            piece = top + PIECE * came
            last.append(send(rows(full, piece, PIECE), rows(full, piece, PIECE), k, place.partner()))
            k += 1
    for copy in last:
        copy.wait_recv()
    for copy in pending:
        copy.wait_send()


N_COPIES = 3 + 9 * 3 + 9 + 12 + 9


def iterate(gram_ref, start_ref, gram_high, gram_low, aug, basis):
    for i in range(8):
        for j in range(i + 1):
            block = gram_ref[first_row(i, j) : first_row(i, j) + 128, :]
            places = [(i, j, block)] if i == j else [(i, j, block), (j, i, block.T)]
            for r, c, value in places:
                where = (slice(128 * r, 128 * r + 128), slice(128 * c, 128 * c + 128))
                gram_high[where], gram_low[where] = split(value)
    basis[...] = start_ref[...]
    n = aug.shape[0]
    shape = (n, n)
    eye = (lax.broadcasted_iota(jnp.int32, shape, 0) == lax.broadcasted_iota(jnp.int32, shape, 1)).astype(F32)

    def step(_, carry):
        bh, bl = split(basis[...])
        both = dg(gram_high[...], jnp.concatenate([bh, bl], axis=1), 1, 0)
        image = both[:, :n] + both[:, n:] + dg(gram_low[...], bh, 1, 0)
        ih, il = split(image)
        both = dg(ih, jnp.concatenate([ih, il], axis=1), 0, 0)
        mixed = both[:, n:]
        aug[:, :n] = both[:, :n] + mixed + mixed.T
        aug[:, n:] = eye
        lower_inverse(aug)
        th, tl = split(aug[:, n:])
        both = dg(ih, jnp.concatenate([th, tl], axis=0), 1, 1)
        basis[...] = both[:, :n] + both[:, n:] + dg(il, th, 1, 1)
        return carry

    lax.fori_loop(0, ITERS, step, 0)


def project(me, basis, fh, fl, core, cols, sems):
    high, low = split(jnp.concatenate([basis[row_block(me ^ d), :] for d in ARRIVAL], axis=0))
    flat = cols.reshape(1024, 128)
    for a in range(0, 8, 2):
        c = slice(128 * a, 128 * a + 256)
        part = dg(high, fh[:, c], 0, 0) + dg(high, fl[:, c], 0, 0) + dg(low, fh[:, c], 0, 0)
        flat[pl.ds(a, 128, stride=8), :] = part[:, :128]
        flat[pl.ds(a + 1, 128, stride=8), :] = part[:, 128:]
    copies = []
    here = pl.ds(pl.multiple_of(8 * me, 8), 8)
    for d in A2A_ORDER:
        peer = me ^ d
        copies.append(push(cols.at[pl.ds(16 * peer, 16)], core.at[:, here, :], sems, d, {"gx": peer}))
    own = pltpu.make_async_copy(cols.at[pl.ds(16 * me, 16)], core.at[:, here, :], sems.at[0, 0])
    own.start()
    return [own] + copies


def tucker_kernel(field, start, core, scaled, *scratch):
    land, fh, fl, part, full, land0, land1, land2, land3, gram_high, gram_low, aug, basis, cols, sems, more, final = scratch
    place = Place()
    me = place.gx
    peers = [{"gx": me ^ d} for d in range(1, 8)] + [place.partner()]
    peers += [place.along("z", e) for e in (1, 2, 3)] + [place.along("x", e) for e in (1, 3)]
    greet(peers)
    gather_products(me, field, part, land, fh, fl, sems)
    reduce_all(place, part, full, land0, land1, land2, land3, more)
    iterate(full, start, gram_high, gram_low, aug, basis)
    copies = project(me, basis, fh, fl, core, cols, final)
    scaled[...] = basis[row_block(me), :] * jnp.sqrt(F32(1024))
    for copy in copies:
        copy.wait()


def body(field, start_basis):
    rows, (order, rank) = field.shape[0], start_basis.shape
    vmem = pl.BlockSpec(memory_space=pltpu.VMEM)
    core, scaled_basis = pl.pallas_call(
        tucker_kernel,
        out_shape=(jax.ShapeDtypeStruct((16, 64, 128), F32), jax.ShapeDtypeStruct((128, 128), F32)),
        in_specs=[pl.BlockSpec(memory_space=pl.ANY), vmem],
        out_specs=(vmem, vmem),
        scratch_shapes=[
            pltpu.VMEM((8, rows, 8, 128), F32),
            pltpu.VMEM((order, order), BF16),
            pltpu.VMEM((order, order), BF16),
            pltpu.VMEM((2 * HALF, 128), F32),
            pltpu.VMEM((2 * HALF, 128), F32),
            pltpu.VMEM((HALF, 128), F32),
            pltpu.VMEM((9 * PIECE, 128), F32),
            pltpu.VMEM((9 * BIT, 128), F32),
            pltpu.VMEM((9 * BIT, 128), F32),
            pltpu.VMEM((order, order), BF16),
            pltpu.VMEM((order, order), BF16),
            pltpu.VMEM((rank, 2 * rank), F32),
            pltpu.VMEM((order, rank), F32),
            pltpu.VMEM((128, 8, 128), F32),
            pltpu.SemaphoreType.DMA((2, 8)),
            pltpu.SemaphoreType.DMA((2, N_COPIES)),
            pltpu.SemaphoreType.DMA((2, 8)),
        ],
        compiler_params=pltpu.CompilerParams(collective_id=0, has_side_effects=True, vmem_limit_bytes=56 << 20),
    )(field, start_basis)
    return (scaled_basis, core)


def solution(mesh):
    placed = (P("gx", "gy", "gz"), P())
    return jax.shard_map(
        body,
        mesh=mesh,
        in_specs=placed,
        out_specs=(P("gx", None), P("gx", "gy", "gz")),
        check_vma=False,
    )
```
